256 devices in a mesh: row: 16 (over z, x_hi), col: 8 (over y, x_lo), tm: 2 (over core).
Axes of the slice: x: 4 (x_hi: 2, x_lo: 2; x = x_hi * 2 + x_lo), y: 4, z: 8, core: 2. Of those that a mesh axis runs over, the one named last changes fastest.
Arguments:
- occ_rows: bfloat16 [2048, 512], P('row', 'col'), may hold values from -1.2578125 to 1.2578125
- occ_cols: bfloat16 [4096, 512], P('col', 'row'), may hold values from -1.2578125 to 1.2578125
- emp_rows: bfloat16 [2048, 512], P('row', 'col'), may hold values from -1.2578125 to 1.2578125
- emp_cols: bfloat16 [4096, 512], P('col', 'row'), may hold values from -1.2578125 to 1.2578125
- occ_gap: float32 [512], replicated, may hold values from 0.05 to 5
- emp_gap: float32 [512], replicated, may hold values from 0.05 to 5
- times: float32 [4], P('tm'), may hold values from 0.08 to 2
- time_weights: float32 [4], P('tm'), may hold values from 1 to 2
- freqs: float32 [4], replicated, may hold values from 0.1 to 4
- aux_rows: bfloat16 [2048, 2048], P('row'), may hold values from -0.1875 to 0.1875
- aux_cols: bfloat16 [4096, 2048], P('col'), may hold values from -0.125 to 0.125
Outputs:
- polarizability: float32 [4, 2048, 2048], P(None, 'row', ('col', 'tm'))
The draws below stay inside these ranges and needn't reach their ends.
All inputs are finite; a program needn't handle non-finite values.
Results may differ from the reference program's by a relative error of at most 0.0033.
Values may be sent and summed in bfloat16 or wider, within the bound.
No kernel may reach another device: no remote copies, remote signals or barrier semaphores. Data moves between devices by JAX's collectives and lax.ppermute only.
A program may use at most 192 MiB of HBM per device.

```python
import math
import jax
import jax.numpy as jnp
from jax import lax

NORB = 512
NAUX = 2048
NT = 4
NW = 4
RD = 128
NR = 2048
NC = 4096


def draw_times(key, part):
    jitter = jax.random.uniform(key, (NT,), jnp.float32)
    fraction = (jnp.arange(NT, dtype=jnp.float32) + 0.25 + 0.5 * jitter) / NT
    return (0.08 * jnp.exp(fraction * math.log(25.0))).astype(jnp.float32)


def raised(entries, rng, source, target, blocks, factor):
    def block_of(position):
        return (jnp.arange(entries.shape[position]) // (entries.shape[position] // blocks)).reshape((-1,) + (1,) * (entries.ndim - 1 - position))

    near = jax.random.permutation(rng, blocks)[block_of(target)]
    second = (block_of(target) + blocks // 2) % blocks
    return jnp.where((block_of(source) == near) | (block_of(source) == second), factor * entries, entries)


def levels(own_key, dims, split, low, high):
    gain, own = 1.0, jax.random.fold_in(own_key, 6)
    for dim, blocks in split:
        steps = jnp.exp(jax.random.uniform(jax.random.fold_in(own, dim), (blocks,), jnp.float32, low / len(split), high / len(split)))
        gain = gain * jnp.repeat(steps, dims[dim] // blocks).reshape([-1 if axis == dim else 1 for axis in range(len(dims))])
    return gain


def bell_draw(key, shape, spread, bound, cuts=(), held_as=jnp.bfloat16):
    result = jax.random.normal(key, shape, jnp.float32) * spread
    if len(cuts) > 0:
        result = levels(key, shape, cuts, -0.22, 0.18) * result
    return jnp.clip(result, min=-bound, max=bound).astype(held_as)


def noise_with(stream_key, extent, spread, most, pieces, heavy, kind=jnp.bfloat16):
    values = spread * jax.random.normal(stream_key, extent, jnp.float32)
    if pieces:
        values = values * levels(stream_key, extent, pieces, -0.22, 0.18)
    return jnp.clip(raised(values, jax.random.fold_in(stream_key, 3), *heavy), -most, most).astype(kind)


def setup_inputs(seed: int = 0) -> dict:
    seeds = jax.random.split(jax.random.key(seed), 12)
    occ_rows = bell_draw(seeds[0], (NR, NORB), 0.21, 1.2578125, ((0, 16), (1, 8)))
    occ_cols = bell_draw(seeds[1], (NC, NORB), 0.21, 1.2578125, ((0, 8), (1, 16)))
    emp_rows = bell_draw(seeds[2], (NR, NORB), 0.21, 1.2578125, ((0, 16), (1, 8)))
    emp_cols = bell_draw(seeds[3], (NC, NORB), 0.21, 1.2578125, ((0, 8), (1, 16)))
    occ_gap = jnp.clip(jnp.exp(jax.random.uniform(seeds[4], (NORB,), jnp.float32, math.log(0.05), math.log(5.0))), 0.05, 5.0)
    emp_gap = jnp.clip(jnp.exp(jax.random.uniform(seeds[5], (NORB,), jnp.float32, math.log(0.05), math.log(5.0))), 0.05, 5.0)
    times = draw_times(jax.random.fold_in(seeds[11], 71), 0)
    time_weights = jnp.clip(1.0 + 1.0 * jax.random.uniform(seeds[7], (NT,), jnp.float32) ** levels(seeds[7], (NT,), ((0, 2),), -0.2, 0.2), 1.0, 2.0)
    freqs = jnp.clip(jnp.exp(jax.random.uniform(seeds[8], (NW,), jnp.float32, math.log(0.1), math.log(4.0))), 0.1, 4.0)
    aux_rows = noise_with(seeds[9], (NR, NAUX), NR ** -0.5, 0.1875, ((0, 16),), (0, 1, 16, 2.0))
    aux_cols = noise_with(seeds[10], (NC, NAUX), NC ** -0.5, 0.125, ((0, 8),), (0, 1, 8, 2.0))
    return {"occ_rows": occ_rows, "occ_cols": occ_cols, "emp_rows": emp_rows, "emp_cols": emp_cols, "occ_gap": occ_gap, "emp_gap": emp_gap, "times": times, "time_weights": time_weights, "freqs": freqs, "aux_rows": aux_rows, "aux_cols": aux_cols}


def reference(occ_rows, occ_cols, emp_rows, emp_cols, occ_gap, emp_gap, times, time_weights, freqs, aux_rows, aux_cols):
    high = lax.Precision.HIGHEST
    occ_col_f = occ_cols.astype(jnp.float32)
    emp_col_f = emp_cols.astype(jnp.float32)
    blocks = occ_rows.shape[0] // RD

    def per_block(left, index):
        start = (index * RD).astype(jnp.int32)
        occ_block = lax.dynamic_slice_in_dim(occ_rows, start, RD, 0).astype(jnp.float32)
        emp_block = lax.dynamic_slice_in_dim(emp_rows, start, RD, 0).astype(jnp.float32)
        aux_block = lax.dynamic_slice_in_dim(aux_rows, start, RD, 0).astype(jnp.float32)

        def per_time(moment):
            occ_scaled = (occ_block * jnp.exp(-occ_gap * moment)[None, :]).astype(jnp.bfloat16)
            occ_scaled = lax.optimization_barrier(occ_scaled).astype(jnp.float32)
            emp_scaled = (emp_block * jnp.exp(-emp_gap * moment)[None, :]).astype(jnp.bfloat16)
            emp_scaled = lax.optimization_barrier(emp_scaled).astype(jnp.float32)
            green_occ = jnp.dot(occ_scaled, occ_col_f.T, precision=high)
            green_emp = jnp.dot(emp_scaled, emp_col_f.T, precision=high)
            chi_time = (green_occ * green_emp).astype(jnp.bfloat16)
            chi_time = lax.optimization_barrier(chi_time).astype(jnp.float32)
            return jnp.dot(aux_block.T, chi_time, precision=high)

        return left + lax.map(per_time, times), None

    start_left = jnp.zeros((NT, NAUX, occ_cols.shape[0]), jnp.float32)
    left, _ = lax.scan(per_block, start_left, jnp.arange(blocks, dtype=jnp.int32))
    projected = jnp.einsum("tpc,cq->tpq", left, aux_cols.astype(jnp.float32), precision=high)
    coef = time_weights[None, :] * jnp.cos(freqs[:, None] * times[None, :])
    return jnp.einsum("wt,tpq->wpq", coef, projected, precision=high)
```

```python
import jax
import jax.numpy as jnp
from jax import lax
from jax.sharding import Mesh
from jax.sharding import PartitionSpec as P

ROW = ("z2", "z1", "z0", "xh")
COL = ("y", "xl")
SWAP = [(0, 1), (1, 0)]
BOTH = [(0, 3), (1, 2), (2, 1), (3, 0)]


def copies_to_all(block, axes):
    size = lax.axis_size(axes)
    return lax.all_to_all(jnp.broadcast_to(block[None], (size, *block.shape)), axes, 0, 0, tiled=True)


def from_partners(make):
    return [
        make(0, 0),
        lax.ppermute(make(0, 1), "xh", SWAP),
        lax.ppermute(make(1, 0), "z0", SWAP),
        lax.ppermute(make(1, 1), ("z0", "xh"), BOTH),
    ]


def per_device(
    occ_rows,
    occ_cols,
    emp_rows,
    emp_cols,
    occ_gap,
    emp_gap,
    times,
    time_weights,
    freqs,
    aux_rows,
    aux_cols,
):
    first = lax.axis_index("tm") == 0

    mine = jnp.stack([times, time_weights])
    other = lax.ppermute(mine, "tm", SWAP)
    lead, tail = jnp.where(first, mine, other), jnp.where(first, other, mine)
    every = jnp.concatenate([lead, tail], axis=1)

    z0, xh = lax.axis_index("z0"), lax.axis_index("xh")
    split = jnp.moveaxis(aux_rows.reshape(128, 4, 4, 128), 2, 0)

    def aux_for(dz, dx):
        return lax.dynamic_index_in_dim(split, 2 * (z0 ^ dz) + (xh ^ dx), 0, keepdims=False).reshape(128, 512)

    aux = from_partners(aux_for)

    rows_a = jnp.where(first, occ_rows, emp_rows).T
    rows_b = jnp.where(first, emp_rows, occ_rows).T
    rows = copies_to_all(jnp.concatenate([rows_a, rows_b], axis=1), COL).reshape(512, 2, 128)
    cols_a = copies_to_all(jnp.where(first, occ_cols, emp_cols).T, ROW).reshape(512, 512)
    cols_b = lax.ppermute(cols_a, "tm", SWAP)

    def green(which, gap, cols):
        factor = jnp.exp(-gap[:, None] * times[None, :])
        scaled = (rows[:, which, None, :].astype(jnp.float32) * factor[:, :, None]).astype(jnp.bfloat16)
        return jnp.einsum("otr,oc->trc", scaled, cols, preferred_element_type=jnp.float32)

    green_a = green(0, jnp.where(first, occ_gap, emp_gap), cols_a)
    green_b = green(1, jnp.where(first, emp_gap, occ_gap), cols_b)
    chi = (green_a * green_b).astype(jnp.bfloat16).reshape(256, 512)

    right = jnp.einsum("mc,cjq->jmq", chi, aux_cols.reshape(512, 8, 256), preferred_element_type=jnp.float32)
    parts = lax.all_to_all(right.astype(jnp.bfloat16), COL, 0, 0, tiled=True)
    summed = jnp.sum(parts.astype(jnp.float32), axis=0).astype(jnp.bfloat16)

    blocks = from_partners(lambda dz, dx: summed)
    proj = sum(
        jnp.einsum("rp,trq->ptq", a, b.reshape(2, 128, 256), preferred_element_type=jnp.float32)
        for a, b in zip(aux, blocks)
    )
    proj = proj.astype(jnp.bfloat16).reshape(4, 128, 2, 2, 128)
    out = jnp.moveaxis(proj, 3, 1).reshape(8, 128, 2, 128)
    got = lax.all_to_all(out, ("z2", "z1", "tm"), 0, 0, tiled=True).reshape(4, 2, 128, 2, 128)
    whole = jnp.sum(got.astype(jnp.float32), axis=0)
    coef = every[1][None, :] * jnp.cos(freqs[:, None] * every[0][None, :])
    return sum(coef[:, t, None, None] * whole[t // 2, :, t % 2][None] for t in range(4))


def solution(mesh):
    torus = Mesh(mesh.devices.reshape(2, 2, 2, 2, 4, 2, 2), (*ROW, *COL, "tm"))
    return jax.shard_map(
        per_device,
        mesh=torus,
        in_specs=(
            P(ROW, COL),
            P(COL, ROW),
            P(ROW, COL),
            P(COL, ROW),
            P(),
            P(),
            P("tm"),
            P("tm"),
            P(),
            P(ROW, None),
            P(COL, None),
        ),
        out_specs=P(None, ROW, (*COL, "tm")),
        check_vma=False,
    )
```

```python
import jax
import jax.numpy as jnp
from jax import lax
from jax.experimental import pallas as pl
from jax.experimental.pallas import tpu as pltpu
from jax.sharding import Mesh
from jax.sharding import PartitionSpec as P

ROW = ("z2", "z1", "z0", "xh")
COL = ("y", "xl")
SWAP = [(0, 1), (1, 0)]
FIRST = ((0,), (0,))


def over_first(a, b):
    return lax.dot_general(a, b, (FIRST, ((), ())), preferred_element_type=jnp.float32)


def right_kernel(place, factor_a, factor_b, *refs):
    rows, (cols_a, cols_b, aux, out, scaled_a, scaled_b, chi) = refs[:8], refs[8:]

    @pl.when(pl.program_id(0) == 0)
    def _():
        for s in range(8):
            at = pl.ds(pl.multiple_of((place[0] ^ s) * 64, 64), 64)
            for kind, factor, scaled in ((0, factor_a, scaled_a), (1, factor_b, scaled_b)):
                for m in range(4):
                    piece = rows[s][:, m * 256 + kind * 128 : m * 256 + kind * 128 + 128]
                    scaled[at, m * 128 : m * 128 + 128] = (piece.astype(jnp.float32) * factor[at, :]).astype(
                        jnp.bfloat16
                    )
        for m in range(4):
            here = slice(m * 128, m * 128 + 128)
            green_a = over_first(scaled_a[:, here], cols_a[...])
            green_b = over_first(scaled_b[:, here], cols_b[...])
            chi[here, :] = (green_a * green_b).astype(jnp.bfloat16)

    out[0] = jnp.dot(chi[...], aux[...], preferred_element_type=jnp.float32).astype(jnp.bfloat16)


def right_parts(place, factor_a, factor_b, rows, cols_a, cols_b, aux_cols):
    whole = lambda *shape: pl.BlockSpec(shape, lambda g, place: (0,) * len(shape))
    return pl.pallas_call(
        right_kernel,
        name="right_parts",
        compiler_params=pltpu.CompilerParams(vmem_limit_bytes=10 * 2**20),
        out_shape=jax.ShapeDtypeStruct((8, 512, 128), jnp.bfloat16),
        grid_spec=pltpu.PrefetchScalarGridSpec(
            num_scalar_prefetch=1,
            grid=(8,),
            in_specs=[whole(512, 128)] * 2
            + [whole(64, 1024)] * 8
            + [whole(512, 512)] * 2
            + [pl.BlockSpec((512, 128), lambda g, place: (0, 2 * g + place[1]))],
            out_specs=pl.BlockSpec((1, 512, 128), lambda g, place: (g, 0, 0)),
            scratch_shapes=[pltpu.VMEM((512, 512), jnp.bfloat16)] * 3,
        ),
        cost_estimate=pl.CostEstimate(flops=1_100_000_000, bytes_accessed=5_000_000, transcendentals=0),
    )(place, factor_a, factor_b, *rows, cols_a, cols_b, aux_cols)


def left_kernel(parts, *refs):
    aux, out = refs[:4], refs[4]
    pieces = []
    for m in range(4):
        here = slice(m * 128, m * 128 + 128)
        total = parts[0, here, :].astype(jnp.float32)
        for j in range(1, 8):
            total += parts[j, here, :].astype(jnp.float32)
        pieces.append(total.astype(jnp.bfloat16))
    for g in range(4):
        made = sum(over_first(pieces[m], aux[m][:, g * 512 : g * 512 + 512]) for m in range(4))
        for h in range(4):
            out[4 * g + h] = made[:, h * 128 : h * 128 + 128].astype(jnp.bfloat16)


def left_parts(parts, aux):
    return pl.pallas_call(
        left_kernel,
        name="left_parts",
        compiler_params=pltpu.CompilerParams(vmem_limit_bytes=8 * 2**20),
        out_shape=jax.ShapeDtypeStruct((16, 128, 128), jnp.bfloat16),
        cost_estimate=pl.CostEstimate(flops=270_000_000, bytes_accessed=3_500_000, transcendentals=0),
    )(parts, *aux)


def mix_kernel(coef, got, out):
    summed = []
    for t in range(4):
        total = got[t].astype(jnp.float32)
        for m in range(1, 4):
            total += got[4 * m + t].astype(jnp.float32)
        summed.append(total.T)
    for w in range(4):
        out[w] = sum(coef[w, t] * summed[t] for t in range(4))


def mix(coef, got):
    return pl.pallas_call(
        mix_kernel,
        name="mix",
        compiler_params=pltpu.CompilerParams(vmem_limit_bytes=8 * 2**20),
        out_shape=jax.ShapeDtypeStruct((4, 128, 128), jnp.float32),
        in_specs=[pl.BlockSpec(memory_space=pltpu.SMEM), pl.BlockSpec(memory_space=pltpu.VMEM)],
    )(coef, got)


def per_device(
    occ_rows,
    occ_cols,
    emp_rows,
    emp_cols,
    occ_gap,
    emp_gap,
    times,
    time_weights,
    freqs,
    aux_rows,
    aux_cols,
):
    core = lax.axis_index("tm")
    first = core == 0

    cols = jnp.where(first, occ_cols, emp_cols).T
    cols_a = lax.all_to_all(jnp.broadcast_to(cols[None], (16, 32, 512)), ROW, 0, 0, tiled=True).reshape(512, 512)

    rows = jnp.concatenate([jnp.where(first, occ_rows, emp_rows).T, jnp.where(first, emp_rows, occ_rows).T], axis=1)
    rows = jnp.concatenate([rows, lax.ppermute(rows, "xh", SWAP)], axis=1)
    rows = jnp.concatenate([rows, lax.ppermute(rows, "z0", SWAP)], axis=1)
    rows = [rows] + [lax.ppermute(rows, COL, [(j, j ^ s) for j in range(8)]) for s in range(1, 8)]
    rows, cols_a = lax.optimization_barrier((rows, cols_a))
    cols_b = lax.ppermute(cols_a, "tm", SWAP)

    aux = [aux_rows, lax.ppermute(aux_rows, "xh", SWAP)]
    aux += [lax.ppermute(a, "z0", SWAP) for a in aux]

    mine = jnp.stack([times, time_weights])
    other = lax.ppermute(mine, "tm", SWAP)
    every = jnp.concatenate([jnp.where(first, mine, other), jnp.where(first, other, mine)], axis=1)
    coef = every[1][None, :] * jnp.cos(freqs[:, None] * every[0][None, :])
    moment = lax.dynamic_index_in_dim(every[0], 2 * lax.axis_index("z0") + lax.axis_index("xh"), keepdims=False)

    def factor(gap):
        return jnp.broadcast_to(jnp.exp(-gap * moment)[:, None], (512, 128))

    place = jnp.stack([lax.axis_index(COL), core]).astype(jnp.int32)
    parts = right_parts(
        place,
        factor(jnp.where(first, occ_gap, emp_gap)),
        factor(jnp.where(first, emp_gap, occ_gap)),
        rows,
        cols_a,
        cols_b,
        aux_cols,
    )
    parts = lax.all_to_all(parts, COL, 0, 0, tiled=True)
    out = lax.all_to_all(left_parts(parts, aux), ROW, 0, 0, tiled=True)
    return mix(coef, out)


def solution(mesh):
    torus = Mesh(mesh.devices.reshape(2, 2, 2, 2, 4, 2, 2), (*ROW, *COL, "tm"))
    return jax.shard_map(
        per_device,
        mesh=torus,
        in_specs=(
            P(ROW, COL),
            P(COL, ROW),
            P(ROW, COL),
            P(COL, ROW),
            P(),
            P(),
            P("tm"),
            P("tm"),
            P(),
            P(ROW, None),
            P(COL, None),
        ),
        out_specs=P(None, ROW, (*COL, "tm")),
        check_vma=False,
    )
```

```python
import jax
import jax.numpy as jnp
from jax import lax
from jax.experimental import pallas as pl
from jax.experimental.pallas import tpu as pltpu
from jax.sharding import Mesh
from jax.sharding import PartitionSpec as P


ROW = ("z2", "z1", "z0", "xh")
COL = ("y2", "y1", "xl")
SWAP = [(0, 1), (1, 0)]
SMALL = pltpu.CompilerParams(vmem_limit_bytes=6 * 2**20)


def exchange(block, axes, mask):
    return lax.ppermute(block, axes, [(i, i ^ mask) for i in range(lax.axis_size(axes))])


def doubled(block, axis):
    other = lax.ppermute(block, axis, SWAP)
    low = lax.axis_index(axis) == 0
    return jnp.concatenate([jnp.where(low, block, other), jnp.where(low, other, block)], axis=0)


def sum_kernel(*refs):
    parts, out = refs[:-1], refs[-1]
    for t in range(4):
        here = slice(t * 128, t * 128 + 128)
        out[:, here] = sum(part[here, :].astype(jnp.float32) for part in parts).astype(jnp.bfloat16)


def summed(parts):
    return pl.pallas_call(
        sum_kernel,
        name="summed",
        out_shape=jax.ShapeDtypeStruct((128, 512), jnp.bfloat16),
        compiler_params=SMALL,
        cost_estimate=pl.CostEstimate(flops=500_000, bytes_accessed=1_300_000, transcendentals=0),
    )(*parts)


def left_kernel(place, *refs):
    aux, right, outs = refs[:4], refs[4:8], refs[8:]
    for e in range(4):
        at = pl.ds(pl.multiple_of((place[0] ^ e) * 128, 128), 128)
        made = sum(jnp.dot(a[at, :], r[...], preferred_element_type=jnp.float32) for a, r in zip(aux, right))
        outs[e][...] = made.astype(outs[e].dtype)


def left_parts(place, aux, right):
    vmem = pl.BlockSpec(memory_space=pltpu.VMEM)
    return pl.pallas_call(
        left_kernel,
        name="left_parts",
        out_shape=[jax.ShapeDtypeStruct((128, 512), jnp.bfloat16 if e else jnp.float32) for e in range(4)],
        in_specs=[pl.BlockSpec(memory_space=pltpu.SMEM)] + [vmem] * 8,
        out_specs=[vmem] * 4,
        compiler_params=SMALL,
        cost_estimate=pl.CostEstimate(flops=270_000_000, bytes_accessed=1_700_000, transcendentals=0),
    )(place, *aux, *right)


def mix_kernel(coef, *refs):
    parts, out = refs[:4], refs[4]
    whole = [sum(part[:, t * 128 : t * 128 + 128].astype(jnp.float32) for part in parts) for t in range(4)]
    for w in range(4):
        out[w] = sum(coef[w, t] * whole[t] for t in range(4))


def mix(coef, parts):
    vmem = pl.BlockSpec(memory_space=pltpu.VMEM)
    return pl.pallas_call(
        mix_kernel,
        name="mix",
        out_shape=jax.ShapeDtypeStruct((4, 128, 128), jnp.float32),
        in_specs=[pl.BlockSpec(memory_space=pltpu.SMEM)] + [vmem] * 4,
        out_specs=vmem,
        compiler_params=SMALL,
    )(coef, *parts)


def per_device(
    occ_rows,
    occ_cols,
    emp_rows,
    emp_cols,
    occ_gap,
    emp_gap,
    times,
    time_weights,
    freqs,
    aux_rows,
    aux_cols,
):
    core = lax.axis_index("tm")
    first = core == 0
    z2, z1, z0, xh = (lax.axis_index(a) for a in ROW)

    cols = jnp.where(first, occ_cols, emp_cols).T
    cols_a = lax.all_to_all(jnp.broadcast_to(cols[None], (16, 32, 512)), ROW, 0, 0, tiled=True).reshape(512, 512)

    rows = jnp.concatenate([jnp.where(first, occ_rows, emp_rows).T, jnp.where(first, emp_rows, occ_rows).T], axis=1)
    mine = jnp.stack([times, time_weights])
    for axis in reversed(COL):
        rows = doubled(rows, axis)
    other = lax.ppermute(mine, "tm", SWAP)

    every = jnp.concatenate([jnp.where(first, mine, other), jnp.where(first, other, mine)], axis=1)
    coef = every[1][None, :] * jnp.cos(freqs[:, None] * every[0][None, :])

    def scaled(piece, gap):
        factor = jnp.exp(-gap[:, None] * every[0][None, :])
        return (piece[:, None, :].astype(jnp.float32) * factor[:, :, None]).astype(jnp.bfloat16)

    scaled_a = scaled(rows[:, :128], jnp.where(first, occ_gap, emp_gap))
    scaled_b = scaled(rows[:, 128:], jnp.where(first, emp_gap, occ_gap))

    turned = aux_rows.T.reshape(2, 2, 2, 2, 128, 128)
    aux = []
    for mask in range(4):
        start = (0, 0, z0 ^ (mask // 2), xh ^ (mask % 2), 0, 0)
        block = lax.dynamic_slice(turned, start, (2, 2, 1, 1, 128, 128)).reshape(512, 128)
        aux.append(exchange(block, ("z0", "xh"), mask) if mask else block)

    here = lax.axis_index(COL)
    near = (0, 1, 2, 6, 3, 7, 4, 5)
    aux_to = [lax.dynamic_slice(aux_cols, (0, (2 * (here ^ s) + core) * 128), (512, 128)) for s in near]

    held = (scaled_a, scaled_b, cols_a, aux, aux_to)
    scaled_a, scaled_b, cols_a, aux, aux_to = lax.optimization_barrier(held)
    cols_b = lax.ppermute(cols_a, "tm", SWAP)
    green_a = jnp.einsum("otr,oc->trc", scaled_a, cols_a, preferred_element_type=jnp.float32)
    green_b = jnp.einsum("otr,oc->trc", scaled_b, cols_b, preferred_element_type=jnp.float32)
    chi = (green_a * green_b).astype(jnp.bfloat16).reshape(512, 512)

    parts = []
    for s, block in zip(near, aux_to):
        part = jnp.dot(chi, block, preferred_element_type=jnp.float32)
        parts.append(exchange(part.astype(jnp.bfloat16), COL, s) if s else part)
    right = summed(parts)
    right = [right] + [exchange(right, ("z0", "xh"), mask) for mask in (1, 2, 3)]
    place = (2 * z2 + z1).astype(jnp.int32).reshape(1)
    parts = left_parts(place, aux, right)
    parts = [parts[0]] + [exchange(parts[e], ("z2", "z1"), e) for e in (1, 2, 3)]
    return mix(coef, parts)


def solution(mesh):
    torus = Mesh(mesh.devices.reshape((2,) * 8), (*ROW, *COL, "tm"))
    return jax.shard_map(
        per_device,
        mesh=torus,
        in_specs=(
            P(ROW, COL),
            P(COL, ROW),
            P(ROW, COL),
            P(COL, ROW),
            P(),
            P(),
            P("tm"),
            P("tm"),
            P(),
            P(ROW, None),
            P(COL, None),
        ),
        out_specs=P(None, ROW, (*COL, "tm")),
        check_vma=False,
    )
```

```python
import jax
import jax.numpy as jnp
from jax import lax
from jax.experimental import pallas as pl
from jax.experimental.pallas import tpu as pltpu
from jax.sharding import Mesh
from jax.sharding import PartitionSpec as P


ROW = ("z2", "z1", "z0", "xh")
COL = ("y2", "y1", "xl")
SWAP = [(0, 1), (1, 0)]
SMALL = pltpu.CompilerParams(vmem_limit_bytes=6 * 2**20)


def exchange(block, axes, mask):
    return lax.ppermute(block, axes, [(i, i ^ mask) for i in range(lax.axis_size(axes))])


def doubled(block, axis):
    other = lax.ppermute(block, axis, SWAP)
    low = lax.axis_index(axis) == 0
    return jnp.concatenate([jnp.where(low, block, other), jnp.where(low, other, block)], axis=0)


def vmem(count):
    return [pl.BlockSpec(memory_space=pltpu.VMEM)] * count


SCALARS = pl.BlockSpec(memory_space=pltpu.SMEM)


def scale_kernel(place, rows, factor_a, factor_b, scaled_a, scaled_b):
    for m2 in range(4):
        ats = [pl.ds(pl.multiple_of(((place[0] ^ m1) * 4 + (place[1] ^ m2)) * 32, 32), 32) for m1 in range(4)]
        block = jnp.concatenate([rows[at, :] for at in ats], axis=0).astype(jnp.float32)
        for kind, factor, scaled in ((0, factor_a, scaled_a), (1, factor_b, scaled_b)):
            piece = block[:, kind * 128 : kind * 128 + 128].T
            gains = jnp.concatenate([factor[at, :] for at in ats], axis=0).T
            for t in range(4):
                made = piece * gains[t : t + 1, :]
                scaled[t * 128 : t * 128 + 128, m2 * 128 : m2 * 128 + 128] = made.astype(jnp.bfloat16)


def scaled_rows(place, rows, factor_a, factor_b):
    return pl.pallas_call(
        scale_kernel,
        name="scaled_rows",
        out_shape=[jax.ShapeDtypeStruct((512, 512), jnp.bfloat16)] * 2,
        in_specs=[SCALARS] + vmem(3),
        out_specs=vmem(2),
        compiler_params=SMALL,
        cost_estimate=pl.CostEstimate(flops=1_000_000, bytes_accessed=1_800_000, transcendentals=0),
    )(place, rows, factor_a, factor_b)


def copy_kernel(core, block, out):
    out[...] = block[...]


def halved(core, aux_cols):
    return pl.pallas_call(
        copy_kernel,
        name="halved",
        out_shape=jax.ShapeDtypeStruct((512, 1024), jnp.bfloat16),
        grid_spec=pltpu.PrefetchScalarGridSpec(
            num_scalar_prefetch=1,
            grid=(8,),
            in_specs=[pl.BlockSpec((512, 128), lambda j, core: (0, 2 * j + core[0]))],
            out_specs=pl.BlockSpec((512, 128), lambda j, core: (0, j)),
        ),
        compiler_params=SMALL,
        cost_estimate=pl.CostEstimate(flops=0, bytes_accessed=2_000_000, transcendentals=0),
    )(core, aux_cols)


def right_kernel(scaled_a, scaled_b, *refs):
    arrived_a, arrived_b, (aux, out, cols_a, cols_b) = refs[:4], refs[4:8], refs[8:]
    for m in range(4):
        cols_a[m * 128 : m * 128 + 128, :] = arrived_a[m][...]
        cols_b[m * 128 : m * 128 + 128, :] = arrived_b[m][...]
    for t in range(4):
        here = slice(t * 128, t * 128 + 128)
        green_a = jnp.dot(scaled_a[here, :], cols_a[...], preferred_element_type=jnp.float32)
        green_b = jnp.dot(scaled_b[here, :], cols_b[...], preferred_element_type=jnp.float32)
        chi = (green_a * green_b).astype(jnp.bfloat16)
        right = jnp.dot(chi, aux[...], preferred_element_type=jnp.float32).astype(jnp.bfloat16)
        for j in range(8):
            out[j, here, :] = right[:, j * 128 : j * 128 + 128]


def right_parts(scaled_a, scaled_b, cols_a, cols_b, aux):
    return pl.pallas_call(
        right_kernel,
        name="right_parts",
        out_shape=jax.ShapeDtypeStruct((8, 512, 128), jnp.bfloat16),
        in_specs=vmem(11),
        out_specs=vmem(1)[0],
        scratch_shapes=[pltpu.VMEM((512, 512), jnp.bfloat16)] * 2,
        compiler_params=pltpu.CompilerParams(vmem_limit_bytes=12 * 2**20),
        cost_estimate=pl.CostEstimate(flops=1_070_000_000, bytes_accessed=5_000_000, transcendentals=0),
    )(scaled_a, scaled_b, *cols_a, *cols_b, aux)


def turn_kernel(place, aux, mine, theirs):
    for blocks, xh in ((mine, place[2]), (theirs, 1 - place[2])):
        for n in range(8):
            at = pl.ds(pl.multiple_of((2 * n + xh) * 128, 128), 128)
            blocks[n] = aux[:, at].T


def turned(place, aux_rows):
    return pl.pallas_call(
        turn_kernel,
        name="turned",
        out_shape=[jax.ShapeDtypeStruct((8, 128, 128), jnp.bfloat16)] * 2,
        in_specs=[SCALARS] + vmem(1),
        out_specs=vmem(2),
        compiler_params=SMALL,
        cost_estimate=pl.CostEstimate(flops=500_000, bytes_accessed=1_000_000, transcendentals=0),
    )(place, aux_rows)


def sum_kernel(parts, out):
    for t in range(4):
        here = slice(t * 128, t * 128 + 128)
        out[:, here] = sum(parts[j, here, :].astype(jnp.float32) for j in range(8)).astype(jnp.bfloat16)


def summed(parts):
    return pl.pallas_call(
        sum_kernel,
        name="summed",
        out_shape=jax.ShapeDtypeStruct((128, 512), jnp.bfloat16),
        in_specs=vmem(1),
        out_specs=vmem(1)[0],
        compiler_params=SMALL,
        cost_estimate=pl.CostEstimate(flops=500_000, bytes_accessed=1_300_000, transcendentals=0),
    )(parts)


def left_kernel(place, mine, xh_aux, z_aux, *refs):
    right, outs, (left, stacked) = refs[:4], refs[4:8], refs[8:]
    for m in range(4):
        stacked[m * 128 : m * 128 + 128, :] = right[m][...]
    for e in range(4):
        p = place[0] ^ e
        blocks = (mine[2 * p + place[3]], xh_aux[2 * p + place[3]], z_aux[0, p], z_aux[1, p])
        for m, block in enumerate(blocks):
            left[e * 128 : e * 128 + 128, m * 128 : m * 128 + 128] = block
    made = jnp.dot(left[...], stacked[...], preferred_element_type=jnp.float32)
    for e in range(4):
        outs[e][...] = made[e * 128 : e * 128 + 128, :].astype(outs[e].dtype)


def left_parts(place, mine, xh_aux, z_aux, right):
    return pl.pallas_call(
        left_kernel,
        name="left_parts",
        out_shape=[jax.ShapeDtypeStruct((128, 512), jnp.bfloat16 if e else jnp.float32) for e in range(4)],
        in_specs=[SCALARS] + vmem(7),
        out_specs=vmem(4),
        scratch_shapes=[pltpu.VMEM((512, 512), jnp.bfloat16)] * 2,
        compiler_params=SMALL,
        cost_estimate=pl.CostEstimate(flops=270_000_000, bytes_accessed=1_700_000, transcendentals=0),
    )(place, mine, xh_aux, z_aux, *right)


def mix_kernel(coef, *refs):
    parts, out = refs[:4], refs[4]
    whole = [sum(part[:, t * 128 : t * 128 + 128].astype(jnp.float32) for part in parts) for t in range(4)]
    for w in range(4):
        out[w] = sum(coef[w, t] * whole[t] for t in range(4))


def mix(coef, parts):
    return pl.pallas_call(
        mix_kernel,
        name="mix",
        out_shape=jax.ShapeDtypeStruct((4, 128, 128), jnp.float32),
        in_specs=[SCALARS] + vmem(4),
        out_specs=vmem(1)[0],
        compiler_params=SMALL,
    )(coef, *parts)


def per_device(
    occ_rows,
    occ_cols,
    emp_rows,
    emp_cols,
    occ_gap,
    emp_gap,
    times,
    time_weights,
    freqs,
    aux_rows,
    aux_cols,
):
    core = lax.axis_index("tm")
    first = core == 0
    z2, z1, z0, xh = (lax.axis_index(a) for a in ROW)
    place = jnp.stack([2 * z2 + z1, 2 * z0 + xh, xh, z0]).astype(jnp.int32)

    cols = jnp.where(first, occ_cols, emp_cols).T
    cols = jnp.concatenate([cols] + [exchange(cols, ("z2", "z1"), m) for m in (1, 2, 3)], axis=0)
    cols_a = [cols] + [exchange(cols, ("z0", "xh"), m) for m in (1, 2, 3)]
    cols_b = [lax.ppermute(c, "tm", SWAP) for c in cols_a]

    rows = jnp.where(first, occ_rows, emp_rows).T, jnp.where(first, emp_rows, occ_rows).T
    rows = jnp.concatenate(rows, axis=1)
    for axis in reversed(COL):
        rows = doubled(rows, axis)

    mine = jnp.stack([times, time_weights])
    other = lax.ppermute(mine, "tm", SWAP)
    every = jnp.concatenate([jnp.where(first, mine, other), jnp.where(first, other, mine)], axis=1)
    coef = every[1][None, :] * jnp.cos(freqs[:, None] * every[0][None, :])

    moments = jnp.tile(every[0], 32)
    factor_a = jnp.exp(-jnp.where(first, occ_gap, emp_gap)[:, None] * moments[None, :])
    factor_b = jnp.exp(-jnp.where(first, emp_gap, occ_gap)[:, None] * moments[None, :])
    scaled_a, scaled_b = scaled_rows(place, rows, factor_a, factor_b)

    mine, theirs = turned(place, aux_rows)
    xh_aux = exchange(theirs, "xh", 1)

    parts = right_parts(scaled_a, scaled_b, cols_a, cols_b, halved(core.astype(jnp.int32).reshape(1), aux_cols))
    parts = lax.all_to_all(parts, COL, 0, 0, tiled=True)

    z_aux = jnp.stack([mine, xh_aux]).reshape(2, 4, 2, 128, 128)
    z_aux = lax.dynamic_index_in_dim(z_aux, 1 - z0, 2, keepdims=False)
    z_aux = exchange(z_aux, "z0", 1)

    right = summed(parts)
    right = [right] + [exchange(right, ("z0", "xh"), m) for m in (1, 2, 3)]
    parts = left_parts(place, mine, xh_aux, z_aux, right)
    parts = [parts[0]] + [exchange(parts[e], ("z2", "z1"), e) for e in (1, 2, 3)]
    return mix(coef, parts)


def solution(mesh):
    torus = Mesh(mesh.devices.reshape((2,) * 8), (*ROW, *COL, "tm"))
    return jax.shard_map(
        per_device,
        mesh=torus,
        in_specs=(
            P(ROW, COL),
            P(COL, ROW),
            P(ROW, COL),
            P(COL, ROW),
            P(),
            P(),
            P("tm"),
            P("tm"),
            P(),
            P(ROW, None),
            P(COL, None),
        ),
        out_specs=P(None, ROW, (*COL, "tm")),
        check_vma=False,
    )
```

```python
import jax
import jax.numpy as jnp
from jax import lax
from jax.experimental import pallas as pl
from jax.experimental.pallas import tpu as pltpu
from jax.sharding import Mesh
from jax.sharding import PartitionSpec as P


ROW = ("z2", "z1", "z0", "xh")
COL = ("y2", "y1", "xl")
SWAP = [(0, 1), (1, 0)]
SMALL = pltpu.CompilerParams(vmem_limit_bytes=6 * 2**20)

NEAR = (1, 2, 6, 3, 7, 4, 5, 0)


def exchange(block, axes, mask):
    return lax.ppermute(block, axes, [(i, i ^ mask) for i in range(lax.axis_size(axes))])


def doubled(block, axis):
    other = lax.ppermute(block, axis, SWAP)
    low = lax.axis_index(axis) == 0
    return jnp.concatenate([jnp.where(low, block, other), jnp.where(low, other, block)], axis=0)


def vmem(count):
    return [pl.BlockSpec(memory_space=pltpu.VMEM)] * count


SCALARS = pl.BlockSpec(memory_space=pltpu.SMEM)


def index_over(*axes):
    place = 0
    for axis in axes:
        place = 2 * place + lax.axis_index(axis)
    return place


def scale_kernel(mine, other, gap_0, gap_1, rows, aux_cols, scaled_0, scaled_1, aux_to, landed):
    core, here = lax.axis_index("tm"), index_over(*COL)
    fetches = []
    for g, s in enumerate(NEAR):
        block = aux_cols.at[:, pl.ds(pl.multiple_of((2 * (here ^ s) + core) * 128, 128), 128)]
        fetches.append(pltpu.make_async_copy(block, aux_to.at[g], landed.at[g]))
        fetches[g].start()

    first, outer, inner = core == 0, index_over("z2", "z1"), index_over("z0", "xh")
    times = [jnp.where(first == low, mine[i], other[i]) for low in (True, False) for i in range(2)]
    lane = lax.broadcasted_iota(jnp.int32, (1, 128), 1) // 32
    for m2 in range(4):
        ats = [pl.ds(pl.multiple_of(((outer ^ m1) * 4 + (inner ^ m2)) * 32, 32), 32) for m1 in range(4)]
        block = jnp.concatenate([rows[at, :] for at in ats], axis=0).astype(jnp.float32)
        gaps = [jnp.zeros((1, 128), jnp.float32)] * 2
        for m1 in range(4):
            at = pl.ds(outer ^ m1, 1)
            shift = ((m1 - (inner ^ m2)) & 3) * 32
            for kind, gap in enumerate((gap_0, gap_1)):
                gaps[kind] = jnp.where(lane == m1, pltpu.roll(gap[at, :], shift, 1), gaps[kind])
        for kind, scaled in enumerate((scaled_0, scaled_1)):
            piece = block[:, kind * 128 : kind * 128 + 128].T
            gap = jnp.where(first, gaps[kind], gaps[1 - kind])
            for t in range(4):
                made = piece * jnp.exp(-gap * times[t])
                scaled[t * 128 : t * 128 + 128, m2 * 128 : m2 * 128 + 128] = made.astype(jnp.bfloat16)
    for fetch in fetches:
        fetch.wait()


def scaled_rows(mine, other, occ_gap, emp_gap, rows, aux_cols):
    return pl.pallas_call(
        scale_kernel,
        name="scaled_rows",
        out_shape=[jax.ShapeDtypeStruct((512, 512), jnp.bfloat16)] * 2
        + [jax.ShapeDtypeStruct((8, 512, 128), jnp.bfloat16)],
        in_specs=[SCALARS] * 2 + vmem(3) + [pl.BlockSpec(memory_space=pltpu.HBM)],
        out_specs=vmem(3),
        scratch_shapes=[pltpu.SemaphoreType.DMA((8,))],
        compiler_params=SMALL,
        cost_estimate=pl.CostEstimate(flops=1_000_000, bytes_accessed=3_800_000, transcendentals=0),
    )(mine, other, occ_gap.reshape(4, 128), emp_gap.reshape(4, 128), rows, aux_cols)


def chi_kernel(scaled_a, scaled_b, *refs):
    arrived_a, arrived_b, (chi, cols_a, cols_b) = refs[:4], refs[4:8], refs[8:]
    for m in range(4):
        cols_a[m * 128 : m * 128 + 128, :] = arrived_a[m][...]
        cols_b[m * 128 : m * 128 + 128, :] = arrived_b[m][...]
    for t in range(4):
        here = slice(t * 128, t * 128 + 128)
        green_a = jnp.dot(scaled_a[here, :], cols_a[...], preferred_element_type=jnp.float32)
        green_b = jnp.dot(scaled_b[here, :], cols_b[...], preferred_element_type=jnp.float32)
        chi[here, :] = (green_a * green_b).astype(jnp.bfloat16)


def chi_times(scaled_a, scaled_b, cols_a, cols_b):
    return pl.pallas_call(
        chi_kernel,
        name="chi_times",
        out_shape=jax.ShapeDtypeStruct((512, 512), jnp.bfloat16),
        in_specs=vmem(10),
        out_specs=vmem(1)[0],
        scratch_shapes=[pltpu.VMEM((512, 512), jnp.bfloat16)] * 2,
        compiler_params=SMALL,
        cost_estimate=pl.CostEstimate(flops=540_000_000, bytes_accessed=3_000_000, transcendentals=0),
    )(scaled_a, scaled_b, *cols_a, *cols_b)


def turn_kernel(aux, mine, theirs):
    here = lax.axis_index("xh")
    for blocks, xh in ((mine, here), (theirs, 1 - here)):
        for n in range(8):
            at = pl.ds(pl.multiple_of((2 * n + xh) * 128, 128), 128)
            blocks[n] = aux[:, at].T


def turned(aux_rows):
    return pl.pallas_call(
        turn_kernel,
        name="turned",
        out_shape=[jax.ShapeDtypeStruct((8, 128, 128), jnp.bfloat16)] * 2,
        in_specs=vmem(1),
        out_specs=vmem(2),
        compiler_params=SMALL,
        cost_estimate=pl.CostEstimate(flops=500_000, bytes_accessed=1_000_000, transcendentals=0),
    )(aux_rows)


def sum_kernel(*refs):
    parts, out = refs[:-1], refs[-1]
    for t in range(4):
        here = slice(t * 128, t * 128 + 128)
        out[:, here] = sum(part[here, :].astype(jnp.float32) for part in parts).astype(jnp.bfloat16)


def summed(parts):
    return pl.pallas_call(
        sum_kernel,
        name="summed",
        out_shape=jax.ShapeDtypeStruct((128, 512), jnp.bfloat16),
        in_specs=vmem(8),
        out_specs=vmem(1)[0],
        compiler_params=SMALL,
        cost_estimate=pl.CostEstimate(flops=500_000, bytes_accessed=1_300_000, transcendentals=0),
    )(*parts)


def left_kernel(mine, xh_aux, z_aux, *refs):
    right, outs, (left, stacked) = refs[:4], refs[4:8], refs[8:]
    for m in range(4):
        stacked[m * 128 : m * 128 + 128, :] = right[m][...]
    here, z0 = index_over("z2", "z1"), lax.axis_index("z0")
    for e in range(4):
        p = here ^ e
        blocks = (mine[2 * p + z0], xh_aux[2 * p + z0], z_aux[0, p], z_aux[1, p])
        for m, block in enumerate(blocks):
            left[e * 128 : e * 128 + 128, m * 128 : m * 128 + 128] = block
    made = jnp.dot(left[...], stacked[...], preferred_element_type=jnp.float32)
    for e in range(4):
        outs[e][...] = made[e * 128 : e * 128 + 128, :].astype(outs[e].dtype)


def left_parts(mine, xh_aux, z_aux, right):
    return pl.pallas_call(
        left_kernel,
        name="left_parts",
        out_shape=[jax.ShapeDtypeStruct((128, 512), jnp.bfloat16 if e else jnp.float32) for e in range(4)],
        in_specs=vmem(7),
        out_specs=vmem(4),
        scratch_shapes=[pltpu.VMEM((512, 512), jnp.bfloat16)] * 2,
        compiler_params=SMALL,
        cost_estimate=pl.CostEstimate(flops=270_000_000, bytes_accessed=1_700_000, transcendentals=0),
    )(mine, xh_aux, z_aux, *right)


def mix_kernel(coef, *refs):
    parts, out = refs[:4], refs[4]
    whole = [sum(part[:, t * 128 : t * 128 + 128].astype(jnp.float32) for part in parts) for t in range(4)]
    for w in range(4):
        out[w] = sum(coef[w, t] * whole[t] for t in range(4))


def mix(coef, parts):
    return pl.pallas_call(
        mix_kernel,
        name="mix",
        out_shape=jax.ShapeDtypeStruct((4, 128, 128), jnp.float32),
        in_specs=[SCALARS] + vmem(4),
        out_specs=vmem(1)[0],
        compiler_params=SMALL,
    )(coef, *parts)


def per_device(
    occ_rows,
    occ_cols,
    emp_rows,
    emp_cols,
    occ_gap,
    emp_gap,
    times,
    time_weights,
    freqs,
    aux_rows,
    aux_cols,
):
    core = lax.axis_index("tm")
    first = core == 0
    z0 = lax.axis_index("z0")

    cols = jnp.where(first, occ_cols, emp_cols).T
    far = exchange(cols, ("z2", "z1"), 2)
    near = [exchange(cols, ("z2", "z1"), m) for m in (1, 3)]
    cols = jnp.concatenate([cols, near[0], far, near[1]], axis=0)
    cols_a = [cols] + [exchange(cols, ("z0", "xh"), m) for m in (1, 2, 3)]
    cols_b = [lax.ppermute(c, "tm", SWAP) for c in cols_a]

    rows = jnp.where(first, occ_rows, emp_rows).T, jnp.where(first, emp_rows, occ_rows).T
    rows = jnp.concatenate(rows, axis=1)
    for axis in reversed(COL):
        rows = doubled(rows, axis)

    other_times = lax.ppermute(times, "tm", SWAP)
    scaled_a, scaled_b, aux_to = scaled_rows(times, other_times, occ_gap, emp_gap, rows, aux_cols)

    mine, theirs = turned(aux_rows)
    xh_aux = exchange(theirs, "xh", 1)

    chi = chi_times(scaled_a, scaled_b, cols_a, cols_b)
    parts = []
    for g, s in enumerate(NEAR):
        part = jnp.dot(chi, aux_to[g], preferred_element_type=jnp.float32)
        parts.append(exchange(part.astype(jnp.bfloat16), COL, s) if s else part)

    z_aux = jnp.stack([mine, xh_aux]).reshape(2, 4, 2, 128, 128)
    z_aux = lax.dynamic_index_in_dim(z_aux, 1 - z0, 2, keepdims=False)
    z_aux = exchange(z_aux, "z0", 1)

    right = summed(parts)
    right = [right] + [exchange(right, ("z0", "xh"), m) for m in (1, 2, 3)]
    parts = left_parts(mine, xh_aux, z_aux, right)
    held = lax.optimization_barrier((parts[0], times, other_times, time_weights, freqs))
    own, times, other_times, time_weights, freqs = held
    parts = [own] + [exchange(parts[e], ("z2", "z1"), e) for e in (1, 2, 3)]
    other_weights = lax.ppermute(time_weights, "tm", SWAP)
    moments = jnp.where(first, jnp.stack([times, other_times]), jnp.stack([other_times, times])).reshape(4)
    weights = jnp.where(first, jnp.stack([time_weights, other_weights]), jnp.stack([other_weights, time_weights]))
    coef = weights.reshape(1, 4) * jnp.cos(freqs[:, None] * moments[None, :])
    return mix(coef, parts)


def solution(mesh):
    torus = Mesh(mesh.devices.reshape((2,) * 8), (*ROW, *COL, "tm"))
    return jax.shard_map(
        per_device,
        mesh=torus,
        in_specs=(
            P(ROW, COL),
            P(COL, ROW),
            P(ROW, COL),
            P(COL, ROW),
            P(),
            P(),
            P("tm"),
            P("tm"),
            P(),
            P(ROW, None),
            P(COL, None),
        ),
        out_specs=P(None, ROW, (*COL, "tm")),
        check_vma=False,
    )
```

```python
import jax
import jax.numpy as jnp
from jax import lax
from jax.experimental import pallas as pl
from jax.experimental.pallas import tpu as pltpu
from jax.sharding import Mesh
from jax.sharding import PartitionSpec as P


ROW = ("z2", "z1", "z0", "xh")
COL = ("y2", "y1", "xl")
SWAP = [(0, 1), (1, 0)]
SMALL = pltpu.CompilerParams(vmem_limit_bytes=6 * 2**20)

NEAR = (1, 2, 6, 3, 7, 4, 5, 0)


def exchange(block, axes, mask):
    return lax.ppermute(block, axes, [(i, i ^ mask) for i in range(lax.axis_size(axes))])


def doubled(block, axis):
    other = exchange(block, ("y2", "y1"), 3) if axis == "y2" else exchange(block, (axis,), 1)
    low = lax.axis_index(axis) == 0
    return jnp.concatenate([jnp.where(low, block, other), jnp.where(low, other, block)], axis=0)


def vmem(count):
    return [pl.BlockSpec(memory_space=pltpu.VMEM)] * count


SCALARS = pl.BlockSpec(memory_space=pltpu.SMEM)


def index_over(*axes):
    place = 0
    for axis in axes:
        place = 2 * place + lax.axis_index(axis)
    return place


def scale_kernel(mine, other, gap_0, gap_1, rows, scaled_0, scaled_1):
    core = lax.axis_index("tm")
    first, outer, inner = core == 0, index_over("z2", "z1"), index_over("z0", "xh")
    times = [jnp.where(first == low, mine[i], other[i]) for low in (True, False) for i in range(2)]
    lane = lax.broadcasted_iota(jnp.int32, (1, 128), 1) // 32
    for m2 in range(4):
        ats = [pl.ds(pl.multiple_of(((outer ^ m1) * 4 + (inner ^ m2)) * 32, 32), 32) for m1 in range(4)]
        block = jnp.concatenate([rows[at, :] for at in ats], axis=0).astype(jnp.float32)
        gaps = [jnp.zeros((1, 128), jnp.float32)] * 2
        for m1 in range(4):
            at = pl.ds(outer ^ m1, 1)
            shift = ((m1 - (inner ^ m2)) & 3) * 32
            for kind, gap in enumerate((gap_0, gap_1)):
                gaps[kind] = jnp.where(lane == m1, pltpu.roll(gap[at, :], shift, 1), gaps[kind])
        for kind, scaled in enumerate((scaled_0, scaled_1)):
            piece = block[:, kind * 128 : kind * 128 + 128].T
            gap = jnp.where(first, gaps[kind], gaps[1 - kind])
            for t in range(4):
                made = piece * jnp.exp(-gap * times[t])
                scaled[t * 128 : t * 128 + 128, m2 * 128 : m2 * 128 + 128] = made.astype(jnp.bfloat16)


def scaled_rows(mine, other, occ_gap, emp_gap, rows):
    return pl.pallas_call(
        scale_kernel,
        name="scaled_rows",
        out_shape=[jax.ShapeDtypeStruct((512, 512), jnp.bfloat16)] * 2,
        in_specs=[SCALARS] * 2 + vmem(3),
        out_specs=vmem(2),
        compiler_params=SMALL,
        cost_estimate=pl.CostEstimate(flops=1_000_000, bytes_accessed=3_800_000, transcendentals=0),
    )(mine, other, occ_gap.reshape(4, 128), emp_gap.reshape(4, 128), rows)


def chi_kernel(scaled_a, scaled_b, *refs):
    arrived_a, arrived_b, (chi, cols_a, cols_b) = refs[:4], refs[4:8], refs[8:]
    for m in range(4):
        cols_a[m * 128 : m * 128 + 128, :] = arrived_a[m][...]
        cols_b[m * 128 : m * 128 + 128, :] = arrived_b[m][...]
    for t in range(4):
        here = slice(t * 128, t * 128 + 128)
        green_a = jnp.dot(scaled_a[here, :], cols_a[...], preferred_element_type=jnp.float32)
        green_b = jnp.dot(scaled_b[here, :], cols_b[...], preferred_element_type=jnp.float32)
        chi[here, :] = (green_a * green_b).astype(jnp.bfloat16)


def chi_times(scaled_a, scaled_b, cols_a, cols_b):
    return pl.pallas_call(
        chi_kernel,
        name="chi_times",
        out_shape=jax.ShapeDtypeStruct((512, 512), jnp.bfloat16),
        in_specs=vmem(10),
        out_specs=vmem(1)[0],
        scratch_shapes=[pltpu.VMEM((512, 512), jnp.bfloat16)] * 2,
        compiler_params=SMALL,
        cost_estimate=pl.CostEstimate(flops=540_000_000, bytes_accessed=3_000_000, transcendentals=0),
    )(scaled_a, scaled_b, *cols_a, *cols_b)


def turn_kernel(aux, aux_cols, mine, theirs, aux_to, landed):
    core, owner = lax.axis_index("tm"), index_over(*COL)
    fetches = []
    for g, s in enumerate(NEAR):
        block = aux_cols.at[:, pl.ds(pl.multiple_of((2 * (owner ^ s) + core) * 128, 128), 128)]
        fetches.append(pltpu.make_async_copy(block, aux_to.at[g], landed.at[g]))
        fetches[g].start()
    here = lax.axis_index("xh")
    for blocks, xh in ((mine, here), (theirs, 1 - here)):
        for n in range(8):
            at = pl.ds(pl.multiple_of((2 * n + xh) * 128, 128), 128)
            blocks[n] = aux[:, at].T
    for fetch in fetches:
        fetch.wait()


def turned(aux_rows, aux_cols):
    return pl.pallas_call(
        turn_kernel,
        name="turned",
        out_shape=[jax.ShapeDtypeStruct((8, 128, 128), jnp.bfloat16)] * 2
        + [jax.ShapeDtypeStruct((8, 512, 128), jnp.bfloat16)],
        in_specs=vmem(1) + [pl.BlockSpec(memory_space=pltpu.HBM)],
        out_specs=vmem(3),
        scratch_shapes=[pltpu.SemaphoreType.DMA((8,))],
        compiler_params=SMALL,
        cost_estimate=pl.CostEstimate(flops=500_000, bytes_accessed=1_000_000, transcendentals=0),
    )(aux_rows, aux_cols)


def sum_kernel(*refs):
    parts, out = refs[:-1], refs[-1]
    for t in range(4):
        here = slice(t * 128, t * 128 + 128)
        out[:, here] = sum(part[here, :].astype(jnp.float32) for part in parts).astype(jnp.bfloat16)


def summed(parts):
    return pl.pallas_call(
        sum_kernel,
        name="summed",
        out_shape=jax.ShapeDtypeStruct((128, 512), jnp.bfloat16),
        in_specs=vmem(8),
        out_specs=vmem(1)[0],
        compiler_params=SMALL,
        cost_estimate=pl.CostEstimate(flops=500_000, bytes_accessed=1_300_000, transcendentals=0),
    )(*parts)


def left_kernel(mine, xh_aux, z_aux, *refs):
    right, outs, (left, stacked) = refs[:4], refs[4:8], refs[8:]
    for m in range(4):
        stacked[m * 128 : m * 128 + 128, :] = right[m][...]
    here, z0 = index_over("z2", "z1"), lax.axis_index("z0")
    for e in range(4):
        p = here ^ e
        blocks = (mine[2 * p + z0], xh_aux[2 * p + z0], z_aux[0, p], z_aux[1, p])
        for m, block in enumerate(blocks):
            left[e * 128 : e * 128 + 128, m * 128 : m * 128 + 128] = block
    made = jnp.dot(left[...], stacked[...], preferred_element_type=jnp.float32)
    for e in range(4):
        outs[e][...] = made[e * 128 : e * 128 + 128, :].astype(outs[e].dtype)


def left_parts(mine, xh_aux, z_aux, right):
    return pl.pallas_call(
        left_kernel,
        name="left_parts",
        out_shape=[jax.ShapeDtypeStruct((128, 512), jnp.bfloat16 if e else jnp.float32) for e in range(4)],
        in_specs=vmem(7),
        out_specs=vmem(4),
        scratch_shapes=[pltpu.VMEM((512, 512), jnp.bfloat16)] * 2,
        compiler_params=SMALL,
        cost_estimate=pl.CostEstimate(flops=270_000_000, bytes_accessed=1_700_000, transcendentals=0),
    )(mine, xh_aux, z_aux, *right)


def mix_kernel(coef, *refs):
    parts, out = refs[:4], refs[4]
    whole = [sum(part[:, t * 128 : t * 128 + 128].astype(jnp.float32) for part in parts) for t in range(4)]
    for w in range(4):
        out[w] = sum(coef[w, t] * whole[t] for t in range(4))


def mix(coef, parts):
    return pl.pallas_call(
        mix_kernel,
        name="mix",
        out_shape=jax.ShapeDtypeStruct((4, 128, 128), jnp.float32),
        in_specs=[SCALARS] + vmem(4),
        out_specs=vmem(1)[0],
        compiler_params=SMALL,
    )(coef, *parts)


def per_device(
    occ_rows,
    occ_cols,
    emp_rows,
    emp_cols,
    occ_gap,
    emp_gap,
    times,
    time_weights,
    freqs,
    aux_rows,
    aux_cols,
):
    core = lax.axis_index("tm")
    first = core == 0
    z0 = lax.axis_index("z0")

    cols = jnp.where(first, occ_cols, emp_cols).T
    far = exchange(cols, ("z2", "z1"), 2)
    near = [exchange(cols, ("z2", "z1"), m) for m in (1, 3)]
    cols = jnp.concatenate([cols, near[0], far, near[1]], axis=0)
    cols_a = [cols] + [exchange(cols, ("z0", "xh"), m) for m in (1, 2, 3)]
    cols_b = [lax.ppermute(c, "tm", SWAP) for c in cols_a]

    rows = jnp.where(first, occ_rows, emp_rows).T, jnp.where(first, emp_rows, occ_rows).T
    rows = jnp.concatenate(rows, axis=1)
    for axis in reversed(COL):
        rows = doubled(rows, axis)

    other_times = lax.ppermute(times, "tm", SWAP)
    other_weights = lax.ppermute(time_weights, "tm", SWAP)
    scaled_a, scaled_b = scaled_rows(times, other_times, occ_gap, emp_gap, rows)

    mine, theirs, aux_to = turned(aux_rows, aux_cols)
    xh_aux = exchange(theirs, "xh", 1)

    chi = chi_times(scaled_a, scaled_b, cols_a, cols_b)
    parts = []
    for g, s in enumerate(NEAR):
        part = jnp.dot(chi, aux_to[g], preferred_element_type=jnp.float32)
        parts.append(exchange(part.astype(jnp.bfloat16), COL, s) if s else part)

    z_aux = jnp.stack([mine, xh_aux]).reshape(2, 4, 2, 128, 128)
    z_aux = lax.dynamic_index_in_dim(z_aux, 1 - z0, 2, keepdims=False)
    z_aux = exchange(z_aux, "z0", 1)

    right = summed(parts)
    right = [right] + [exchange(right, ("z0", "xh"), m) for m in (1, 2, 3)]
    parts = left_parts(mine, xh_aux, z_aux, right)
    held = lax.optimization_barrier((parts[0], times, other_times, time_weights, other_weights, freqs))
    own, times, other_times, time_weights, other_weights, freqs = held
    parts = [own] + [exchange(parts[e], ("z2", "z1"), e) for e in (1, 2, 3)]
    moments = jnp.where(first, jnp.stack([times, other_times]), jnp.stack([other_times, times])).reshape(4)
    weights = jnp.where(first, jnp.stack([time_weights, other_weights]), jnp.stack([other_weights, time_weights]))
    coef = weights.reshape(1, 4) * jnp.cos(freqs[:, None] * moments[None, :])
    return mix(coef, parts)


def solution(mesh):
    torus = Mesh(mesh.devices.reshape((2,) * 8), (*ROW, *COL, "tm"))
    return jax.shard_map(
        per_device,
        mesh=torus,
        in_specs=(
            P(ROW, COL),
            P(COL, ROW),
            P(ROW, COL),
            P(COL, ROW),
            P(),
            P(),
            P("tm"),
            P("tm"),
            P(),
            P(ROW, None),
            P(COL, None),
        ),
        out_specs=P(None, ROW, (*COL, "tm")),
        check_vma=False,
    )
```

```python
import jax
import jax.numpy as jnp
from jax import lax
from jax.experimental import pallas as pl
from jax.experimental.pallas import tpu as pltpu
from jax.sharding import Mesh
from jax.sharding import PartitionSpec as P


ROW = ("z2", "z1", "z0", "xh")
COL = ("y2", "y1", "xl")
SWAP = [(0, 1), (1, 0)]
SMALL = pltpu.CompilerParams(vmem_limit_bytes=6 * 2**20)

NEAR = (1, 2, 6, 3, 7, 4, 5, 0)


def exchange(block, axes, mask):
    return lax.ppermute(block, axes, [(i, i ^ mask) for i in range(lax.axis_size(axes))])


def doubled(block, axis):
    other = exchange(block, ("y2", "y1"), 3) if axis == "y2" else exchange(block, (axis,), 1)
    low = lax.axis_index(axis) == 0
    return jnp.concatenate([jnp.where(low, block, other), jnp.where(low, other, block)], axis=0)


def vmem(count):
    return [pl.BlockSpec(memory_space=pltpu.VMEM)] * count


SCALARS = pl.BlockSpec(memory_space=pltpu.SMEM)


def index_over(*axes):
    place = 0
    for axis in axes:
        place = 2 * place + lax.axis_index(axis)
    return place


def scale_kernel(mine, other, gap_0, gap_1, rows, scaled_0, scaled_1):
    core = lax.axis_index("tm")
    first, outer, inner = core == 0, index_over("z2", "z1"), index_over("z0", "xh")
    times = [jnp.where(first == low, mine[i], other[i]) for low in (True, False) for i in range(2)]
    lane = lax.broadcasted_iota(jnp.int32, (1, 128), 1) // 32
    for m2 in range(4):
        ats = [pl.ds(pl.multiple_of(((outer ^ m1) * 4 + (inner ^ m2)) * 32, 32), 32) for m1 in range(4)]
        block = jnp.concatenate([rows[at, :] for at in ats], axis=0).astype(jnp.float32)
        gaps = [jnp.zeros((1, 128), jnp.float32)] * 2
        for m1 in range(4):
            at = pl.ds(outer ^ m1, 1)
            shift = ((m1 - (inner ^ m2)) & 3) * 32
            for kind, gap in enumerate((gap_0, gap_1)):
                gaps[kind] = jnp.where(lane == m1, pltpu.roll(gap[at, :], shift, 1), gaps[kind])
        for kind, scaled in enumerate((scaled_0, scaled_1)):
            piece = block[:, kind * 128 : kind * 128 + 128].T
            gap = jnp.where(first, gaps[kind], gaps[1 - kind])
            for t in range(4):
                made = piece * jnp.exp(-gap * times[t])
                scaled[t * 128 : t * 128 + 128, m2 * 128 : m2 * 128 + 128] = made.astype(jnp.bfloat16)


def scaled_rows(mine, other, occ_gap, emp_gap, rows):
    return pl.pallas_call(
        scale_kernel,
        name="scaled_rows",
        out_shape=[jax.ShapeDtypeStruct((512, 512), jnp.bfloat16)] * 2,
        in_specs=[SCALARS] * 2 + vmem(3),
        out_specs=vmem(2),
        compiler_params=SMALL,
        cost_estimate=pl.CostEstimate(flops=1_000_000, bytes_accessed=3_800_000, transcendentals=0),
    )(mine, other, occ_gap.reshape(4, 128), emp_gap.reshape(4, 128), rows)


def chi_kernel(scaled_a, scaled_b, *refs):
    arrived_a, arrived_b, (aux, chi, *parts, cols_a, cols_b) = refs[:4], refs[4:8], refs[8:]
    for m in range(4):
        cols_a[m * 128 : m * 128 + 128, :] = arrived_a[m][...]
        cols_b[m * 128 : m * 128 + 128, :] = arrived_b[m][...]
    for t in range(4):
        here = slice(t * 128, t * 128 + 128)
        green_a = jnp.dot(scaled_a[here, :], cols_a[...], preferred_element_type=jnp.float32)
        green_b = jnp.dot(scaled_b[here, :], cols_b[...], preferred_element_type=jnp.float32)
        chi[here, :] = (green_a * green_b).astype(jnp.bfloat16)
    for g, part in enumerate(parts):
        part[...] = jnp.dot(chi[...], aux[g], preferred_element_type=jnp.float32).astype(jnp.bfloat16)


def chi_times(scaled_a, scaled_b, cols_a, cols_b, aux_to):
    return pl.pallas_call(
        chi_kernel,
        name="chi_times",
        out_shape=[jax.ShapeDtypeStruct((512, 512), jnp.bfloat16)]
        + [jax.ShapeDtypeStruct((512, 128), jnp.bfloat16)] * 2,
        in_specs=vmem(11),
        out_specs=vmem(3),
        scratch_shapes=[pltpu.VMEM((512, 512), jnp.bfloat16)] * 2,
        compiler_params=SMALL,
        cost_estimate=pl.CostEstimate(flops=540_000_000, bytes_accessed=3_000_000, transcendentals=0),
    )(scaled_a, scaled_b, *cols_a, *cols_b, aux_to)


def turn_kernel(aux, aux_cols, mine, theirs, aux_to, landed):
    core, owner = lax.axis_index("tm"), index_over(*COL)
    fetches = []
    for g, s in enumerate(NEAR):
        block = aux_cols.at[:, pl.ds(pl.multiple_of((2 * (owner ^ s) + core) * 128, 128), 128)]
        fetches.append(pltpu.make_async_copy(block, aux_to.at[g], landed.at[g]))
        fetches[g].start()
    here = lax.axis_index("xh")
    for blocks, xh in ((mine, here), (theirs, 1 - here)):
        for n in range(8):
            at = pl.ds(pl.multiple_of((2 * n + xh) * 128, 128), 128)
            blocks[n] = aux[:, at].T
    for fetch in fetches:
        fetch.wait()


def turned(aux_rows, aux_cols):
    return pl.pallas_call(
        turn_kernel,
        name="turned",
        out_shape=[jax.ShapeDtypeStruct((8, 128, 128), jnp.bfloat16)] * 2
        + [jax.ShapeDtypeStruct((8, 512, 128), jnp.bfloat16)],
        in_specs=vmem(1) + [pl.BlockSpec(memory_space=pltpu.HBM)],
        out_specs=vmem(3),
        scratch_shapes=[pltpu.SemaphoreType.DMA((8,))],
        compiler_params=SMALL,
        cost_estimate=pl.CostEstimate(flops=500_000, bytes_accessed=1_000_000, transcendentals=0),
    )(aux_rows, aux_cols)


def sum_kernel(*refs):
    parts, out = refs[:-1], refs[-1]
    for t in range(4):
        here = slice(t * 128, t * 128 + 128)
        out[:, here] = sum(part[here, :].astype(jnp.float32) for part in parts).astype(jnp.bfloat16)


def summed(parts):
    return pl.pallas_call(
        sum_kernel,
        name="summed",
        out_shape=jax.ShapeDtypeStruct((128, 512), jnp.bfloat16),
        in_specs=vmem(8),
        out_specs=vmem(1)[0],
        compiler_params=SMALL,
        cost_estimate=pl.CostEstimate(flops=500_000, bytes_accessed=1_300_000, transcendentals=0),
    )(*parts)


def left_kernel(mine, xh_aux, z_aux, *refs):
    right, outs, (left, stacked) = refs[:4], refs[4:8], refs[8:]
    for m in range(4):
        stacked[m * 128 : m * 128 + 128, :] = right[m][...]
    here, z0 = index_over("z2", "z1"), lax.axis_index("z0")
    for e in range(4):
        p = here ^ e
        blocks = (mine[2 * p + z0], xh_aux[2 * p + z0], z_aux[0, p], z_aux[1, p])
        for m, block in enumerate(blocks):
            left[e * 128 : e * 128 + 128, m * 128 : m * 128 + 128] = block
    made = jnp.dot(left[...], stacked[...], preferred_element_type=jnp.float32)
    for e in range(4):
        outs[e][...] = made[e * 128 : e * 128 + 128, :].astype(outs[e].dtype)


def left_parts(mine, xh_aux, z_aux, right):
    return pl.pallas_call(
        left_kernel,
        name="left_parts",
        out_shape=[jax.ShapeDtypeStruct((128, 512), jnp.bfloat16 if e else jnp.float32) for e in range(4)],
        in_specs=vmem(7),
        out_specs=vmem(4),
        scratch_shapes=[pltpu.VMEM((512, 512), jnp.bfloat16)] * 2,
        compiler_params=SMALL,
        cost_estimate=pl.CostEstimate(flops=270_000_000, bytes_accessed=1_700_000, transcendentals=0),
    )(mine, xh_aux, z_aux, *right)


def mix_kernel(coef, *refs):
    parts, out = refs[:4], refs[4]
    whole = [sum(part[:, t * 128 : t * 128 + 128].astype(jnp.float32) for part in parts) for t in range(4)]
    for w in range(4):
        out[w] = sum(coef[w, t] * whole[t] for t in range(4))


def mix(coef, parts):
    return pl.pallas_call(
        mix_kernel,
        name="mix",
        out_shape=jax.ShapeDtypeStruct((4, 128, 128), jnp.float32),
        in_specs=[SCALARS] + vmem(4),
        out_specs=vmem(1)[0],
        compiler_params=SMALL,
    )(coef, *parts)


def per_device(
    occ_rows,
    occ_cols,
    emp_rows,
    emp_cols,
    occ_gap,
    emp_gap,
    times,
    time_weights,
    freqs,
    aux_rows,
    aux_cols,
):
    core = lax.axis_index("tm")
    first = core == 0
    z0 = lax.axis_index("z0")

    cols = jnp.where(first, occ_cols, emp_cols).T
    far = exchange(cols, ("z2", "z1"), 2)
    near = [exchange(cols, ("z2", "z1"), m) for m in (1, 3)]
    cols = jnp.concatenate([cols, near[0], far, near[1]], axis=0)
    cols_a = [cols] + [exchange(cols, ("z0", "xh"), m) for m in (1, 2, 3)]
    cols_b = [lax.ppermute(c, "tm", SWAP) for c in cols_a]

    rows = jnp.where(first, occ_rows, emp_rows).T, jnp.where(first, emp_rows, occ_rows).T
    rows = jnp.concatenate(rows, axis=1)
    for axis in reversed(COL):
        rows = doubled(rows, axis)

    other_times = lax.ppermute(times, "tm", SWAP)
    other_weights = lax.ppermute(time_weights, "tm", SWAP)
    scaled_a, scaled_b = scaled_rows(times, other_times, occ_gap, emp_gap, rows)

    mine, theirs, aux_to = turned(aux_rows, aux_cols)
    xh_aux = exchange(theirs, "xh", 1)

    chi, *ready = chi_times(scaled_a, scaled_b, cols_a, cols_b, aux_to)
    parts = []
    for g, s in enumerate(NEAR):
        part = ready[g] if g < 2 else jnp.dot(chi, aux_to[g], preferred_element_type=jnp.float32)
        parts.append(exchange(part.astype(jnp.bfloat16), COL, s) if s else part)

    z_aux = jnp.stack([mine, xh_aux]).reshape(2, 4, 2, 128, 128)
    z_aux = lax.dynamic_index_in_dim(z_aux, 1 - z0, 2, keepdims=False)
    z_aux = exchange(z_aux, "z0", 1)

    right = summed(parts)
    right = [right] + [exchange(right, ("z0", "xh"), m) for m in (1, 2, 3)]
    parts = left_parts(mine, xh_aux, z_aux, right)
    held = lax.optimization_barrier((parts[0], times, other_times, time_weights, other_weights, freqs))
    own, times, other_times, time_weights, other_weights, freqs = held
    parts = [own] + [exchange(parts[e], ("z2", "z1"), e) for e in (1, 2, 3)]
    moments = jnp.where(first, jnp.stack([times, other_times]), jnp.stack([other_times, times])).reshape(4)
    weights = jnp.where(first, jnp.stack([time_weights, other_weights]), jnp.stack([other_weights, time_weights]))
    coef = weights.reshape(1, 4) * jnp.cos(freqs[:, None] * moments[None, :])
    return mix(coef, parts)


def solution(mesh):
    torus = Mesh(mesh.devices.reshape((2,) * 8), (*ROW, *COL, "tm"))
    return jax.shard_map(
        per_device,
        mesh=torus,
        in_specs=(
            P(ROW, COL),
            P(COL, ROW),
            P(ROW, COL),
            P(COL, ROW),
            P(),
            P(),
            P("tm"),
            P("tm"),
            P(),
            P(ROW, None),
            P(COL, None),
        ),
        out_specs=P(None, ROW, (*COL, "tm")),
        check_vma=False,
    )
```
